32 devices in a mesh: depth: 2 (over core), row: 4 (over y, x), col: 4 (over z).
Axes of the slice: x: 2, y: 2, z: 4, core: 2. Of those that a mesh axis runs over, the one named last changes fastest.
Arguments:
- tile_left: bfloat16 [16, 16, 64, 1024], P('row', 'col'), may hold values from -6 to 6
- tile_right: bfloat16 [16, 16, 64, 1024], P('row', 'col'), may hold values from -6 to 6
- row_left: bfloat16 [16, 8, 64, 1024], P('row', 'depth', None, 'col'), may hold values from -6 to 6
- row_right: bfloat16 [16, 8, 64, 1024], P('row', 'depth', None, 'col'), may hold values from -0.1875 to 0.1875
- col_left: bfloat16 [16, 8, 64, 1024], P('col', 'depth', None, 'row'), may hold values from -6 to 6
- col_right: bfloat16 [16, 8, 64, 1024], P('col', 'depth', None, 'row'), may hold values from -0.1875 to 0.1875
- row_mask: int32 [16, 8], P('row', 'depth'), may hold values 0 or 1
- col_mask: int32 [16, 8], P('col', 'depth'), may hold values 0 or 1
- sketch: bfloat16 [64, 1024], replicated, may hold values from -1 to 1
Outputs:
- new_left: float32 [16, 16, 64, 1024], P('row', 'col', 'depth')
- new_right: float32 [16, 16, 64, 1024], P('row', 'col', 'depth')
The draws below stay inside these ranges and needn't reach their ends.
All inputs are finite; a program needn't handle non-finite values. No bound on the sum of `row_mask` or of `col_mask` on one device may be relied on, other than what follows from the above.
Results may differ from the reference program's by a relative error of at most 0.0003.
Values may be sent and summed in bfloat16 or wider, within the bound.
No kernel may reach another device: no remote copies, remote signals or barrier semaphores. Data moves between devices by JAX's collectives and lax.ppermute only.
A program may use at most 64 MiB of HBM per device.

```python
import math
import jax
import jax.numpy as jnp
from jax import lax

NB = 1024
K = 64
TR = 16
TC = 16
PANEL = 8


def draw_sketch(key, part):
    key_rows = jax.random.fold_in(key, 11)
    key_gains = jax.random.fold_in(key, 12)
    entries = jnp.clip(jax.random.normal(key_rows, (K, NB), jnp.float32), -5.0, 5.0)
    gains = jax.random.uniform(key_gains, (K, 1), jnp.float32, 0.75, 1.25)
    entries = gains * entries / math.sqrt(NB)
    return jnp.clip(entries, -1.0, 1.0).astype(jnp.bfloat16)


def factor_entries(key, shape):
    key_vals = jax.random.fold_in(key, 21)
    entries = jnp.clip(jax.random.normal(key_vals, shape, jnp.float32), -6.0, 6.0)
    return entries.astype(jnp.bfloat16)


def draw_tile_left(key, part):
    return factor_entries(jax.random.fold_in(key, 31), (TR, TC, K, NB))


def draw_tile_right(key, part):
    return factor_entries(jax.random.fold_in(key, 32), (TR, TC, K, NB))


def draw_row_left(key, part):
    return factor_entries(jax.random.fold_in(key, 33), (TR, PANEL, K, NB))


def draw_col_left(key, part):
    return factor_entries(jax.random.fold_in(key, 34), (TC, PANEL, K, NB))


def touch_ends(values, key, least, largest):
    longest = values.shape.index(max(values.shape))
    spots = []
    for shift in (0, 1):
        where = [jax.random.randint(jax.random.fold_in(key, axis), (), 0, length) for axis, length in enumerate(values.shape)]
        where[longest] = (where[longest] + shift) % values.shape[longest]
        spots.append(tuple(where))
    return values.at[spots[0]].set(least).at[spots[1]].set(largest)


def levels(stream_key, dims, pieces, least, high):
    factor_of = 1.0
    for position, blocks in pieces:
        steps = jax.random.uniform(jax.random.fold_in(jax.random.fold_in(stream_key, 6), position), (blocks,), jnp.float32, least / len(pieces), high / len(pieces))
        factor_of = factor_of * jnp.repeat(jnp.exp(steps), dims[position] // blocks).reshape((-1,) + (1,) * (len(dims) - 1 - position))
    return factor_of


def scatter_about(stream_key, dims, width, limit, shards=(), dtype=jnp.bfloat16):
    result = width * jax.random.normal(stream_key, dims, jnp.float32)
    if shards:
        result = result * levels(stream_key, dims, shards, -0.22, 0.18)
    return jnp.clip(result, -limit, limit).astype(dtype)


def setup_inputs(seed: int = 0) -> dict:
    streams_of = jax.random.split(jax.random.key(seed), 10)
    return {
        "tile_left": draw_tile_left(jax.random.fold_in(streams_of[9], 71), 0),
        "tile_right": draw_tile_right(jax.random.fold_in(streams_of[9], 71), 0),
        "row_left": draw_row_left(jax.random.fold_in(streams_of[9], 71), 0),
        "row_right": scatter_about(streams_of[3], (TR, PANEL, K, NB), NB ** -0.5, 0.1875, ((0, 4), (1, 2), (3, 4))),
        "col_left": draw_col_left(jax.random.fold_in(streams_of[9], 71), 0),
        "col_right": scatter_about(streams_of[5], (TC, PANEL, K, NB), NB ** -0.5, 0.1875, ((0, 4), (1, 2), (3, 4))),
        "row_mask": touch_ends((jax.random.randint(streams_of[6], (TR, PANEL), 0, 4) < 3).astype(jnp.int32), jax.random.fold_in(streams_of[6], 1), 0, 1),
        "col_mask": touch_ends((jax.random.randint(streams_of[7], (TC, PANEL), 0, 4) < 3).astype(jnp.int32), jax.random.fold_in(streams_of[7], 1), 0, 1),
        "sketch": draw_sketch(jax.random.fold_in(streams_of[9], 71), 0),
    }


exact_mode = lax.Precision.HIGHEST

def orthonormalize(sketched):
    for repeat in range(2):
        gram_mat = jnp.einsum('jtn,jsn->jts', sketched, sketched, precision=exact_mode)
        factor = jnp.linalg.cholesky(gram_mat)
        sketched = jax.scipy.linalg.solve_triangular(factor, sketched, lower=True)
    return sketched

def reference(tile_left, tile_right, row_left, row_right, col_left, col_right, row_mask, col_mask, sketch):
    sketch_full = sketch.astype(jnp.float32)
    col_left_full = col_left.astype(jnp.float32)
    col_right_full = col_right.astype(jnp.float32)
    col_sketch = jnp.einsum('jksn,tn->jkst', col_left_full, sketch_full, precision=exact_mode)
    col_weight = col_mask.astype(jnp.float32)

    def one_row(items):
        left_row, right_row, mask_row, tile_l, tile_r = items
        left_row = left_row.astype(jnp.float32)
        tile_l = tile_l.astype(jnp.float32)
        tile_r = tile_r.astype(jnp.float32)
        coupling = jnp.einsum('krn,jksn->jkrs', right_row.astype(jnp.float32), col_right_full, precision=exact_mode)
        coupling = coupling * (mask_row.astype(jnp.float32)[None, :] * col_weight)[:, :, None, None]
        mixing = jnp.einsum('jkrs,jkst->jkrt', coupling, col_sketch, precision=exact_mode)
        sketch_right = jnp.einsum('jrn,tn->jrt', tile_r, sketch_full, precision=exact_mode)
        sketched = jnp.einsum('jrt,jrn->jtn', sketch_right, tile_l, precision=exact_mode)
        sketched = sketched - jnp.einsum('jkrt,krn->jtn', mixing, left_row, precision=exact_mode)
        basis = orthonormalize(sketched)
        basis_row = jnp.einsum('jtn,krn->jktr', basis, left_row, precision=exact_mode)
        projected = jnp.einsum('jktr,jkrs->jkts', basis_row, coupling, precision=exact_mode)
        own_part = jnp.einsum('jtn,jrn->jtr', basis, tile_l, precision=exact_mode)
        right_new = jnp.einsum('jtr,jrn->jtn', own_part, tile_r, precision=exact_mode)
        right_new = right_new - jnp.einsum('jkts,jksn->jtn', projected, col_left_full, precision=exact_mode)
        return (basis * math.sqrt(NB), right_new / math.sqrt(NB))
    new_left, new_right = lax.map(one_row, (row_left, row_right, row_mask, tile_left, tile_right))
    return (new_left, new_right)
```

```python
import functools
import math

import jax
import jax.numpy as jnp
from jax import lax
from jax.experimental import pallas as pl
from jax.experimental.pallas import tpu as pltpu
from jax.sharding import PartitionSpec as P


exact_mode = lax.Precision.HIGHEST
F32 = jnp.float32
BF16 = jnp.bfloat16
NT = (((1,), (1,)), ((), ()))
NN = (((1,), (0,)), ((), ()))


def split3(a):
    high = a.astype(BF16)
    rest = a - high.astype(F32)
    mid = rest.astype(BF16)
    low = (rest - mid.astype(F32)).astype(BF16)
    return high, mid, low


def dot1(a, b, dims=NN):
    return lax.dot_general(a, b, dims, preferred_element_type=F32)


def dot3(a, b, dims=NN):
    m = a.shape[0]
    r = dot1(jnp.concatenate(split3(a), axis=0), b, dims)
    return r[:m] + (r[m : 2 * m] + r[2 * m :])


def dot6(a, b, dims=NN):
    m = a.shape[0]
    ah, am, al = split3(a)
    bh, bm, bl = split3(b)
    r = dot1(jnp.concatenate((ah, am, al), axis=0), bh, dims)
    s = dot1(jnp.concatenate((ah, am), axis=0), bm, dims)
    t = dot1(ah, bl, dims)
    return r[:m] + ((r[m : 2 * m] + s[:m]) + (r[2 * m :] + (s[m:] + t)))


def gram6(a):
    m = a.shape[0]
    ah, am, al = split3(a)
    r = dot1(jnp.concatenate((ah, am, al), axis=0), ah, NT)
    s = dot1(am, am, NT)
    cross = r[m : 2 * m] + r[2 * m :]
    return r[:m] + (cross + cross.T + s)


def invert_factors(work, tiles, rank):
    shape = (tiles, 8, 2 * rank)
    sub = lax.broadcasted_iota(jnp.int32, shape, 1)
    row_of = lambda x, a: jnp.broadcast_to(x[:, a : a + 1, :], shape)
    lane_of = lambda x, a: jnp.broadcast_to(x[:, :, a : a + 1], shape)
    for blk in range(rank // 8):
        base = 8 * blk
        q = work[:, base : base + 8, :]
        kept = q
        scale = q
        for a in range(0, 8, 2):
            b = a + 1
            row_a, row_b = row_of(q, a), row_of(q, b)
            col_a, col_b = lane_of(q, base + a), lane_of(q, base + b)
            piv_a, low, piv_b = row_of(col_a, a), row_of(col_a, b), row_of(col_b, b)
            inv_a = 1.0 / piv_a
            ratio = low * inv_a
            row_b = row_b - ratio * row_a
            piv_b = piv_b - ratio * low
            kept = jnp.where(sub == a, row_a, jnp.where(sub == b, row_b, kept))
            scale = jnp.where(sub == a, piv_a, jnp.where(sub == b, piv_b, scale))
            new_b = row_b / piv_b
            new_a = (row_a - low * new_b) * inv_a
            q = q - col_a * new_a - col_b * new_b
            q = jnp.where(sub == a, new_a, jnp.where(sub == b, new_b, q))
        work[:, base : base + 8, :] = kept * lax.rsqrt(scale)
        rows = [row_of(q, a) for a in range(8)]
        for below in range(blk + 1, rank // 8):
            x = work[:, 8 * below : 8 * below + 8, :]
            y = x
            for a in range(8):
                y = y - lane_of(x, base + a) * rows[a]
            work[:, 8 * below : 8 * below + 8, :] = y


def orthonormal_rows(big, work, tiles, rank):
    eye = (
        lax.broadcasted_iota(jnp.int32, (rank, rank), 0)
        == lax.broadcasted_iota(jnp.int32, (rank, rank), 1)
    ).astype(F32)
    for repeat in range(2):
        for t in range(tiles):
            work[t] = jnp.concatenate((gram6(big[t]), eye), axis=1)
        invert_factors(work, tiles, rank)
        for t in range(tiles):
            big[t] = dot6(work[t][:, rank:], big[t])


def coupling_kernel(n_col, n_row, place, rmask, cmask, *refs):
    rr = refs[:n_col]
    cr = refs[n_col : n_col + n_row]
    out, full_a, full_b = refs[n_col + n_row :]
    ti, nk, rank, wa = rr[0].shape
    tj, _, _, wb = cr[0].shape
    for p in range(n_col):
        off = pl.multiple_of(place[p] * wa, wa)
        for i in range(ti):
            for k in range(nk):
                full_a[k, i * rank : (i + 1) * rank, pl.ds(off, wa)] = rr[p][i, k]
    for p in range(n_row):
        off = pl.multiple_of(place[n_col + p] * wb, wb)
        for j in range(tj):
            for k in range(nk):
                full_b[k, j * rank : (j + 1) * rank, pl.ds(off, wb)] = cr[p][j, k]
    lane = lax.broadcasted_iota(jnp.int32, (1, tj * rank), 1) // rank
    for k in range(nk):
        both = dot1(full_a[k], full_b[k], NT)
        cols = jnp.zeros((1, tj * rank), F32)
        for j in range(tj):
            cols = jnp.where(lane == j, cmask[j, k].astype(F32), cols)
        for i in range(ti):
            rows = slice(i * rank, (i + 1) * rank)
            out[k, rows, :] = both[rows, :] * (cols * rmask[i, k].astype(F32))


def tiles_kernel(n_col, n_row, place, *refs):
    n_in = 2 * n_col + 2 * n_row + 5
    rl = refs[:n_col], refs[n_col : 2 * n_col]
    cl = refs[2 * n_col : 2 * n_col + n_row], refs[2 * n_col + n_row : 2 * n_col + 2 * n_row]
    cpl = refs[n_in - 5], refs[n_in - 4]
    tl, tr, sk = refs[n_in - 3 : n_in]
    new_left, new_right = refs[n_in : n_in + 2]
    row_full, col_full, csk, mix, big, work, proj = refs[n_in + 2 :]
    ti, nk, rank, wa = rl[0][0].shape
    tj, _, _, wb = cl[0][0].shape
    nb = sk.shape[1]
    half = new_left.shape[2]
    depth_at = place[n_col + n_row]
    for side in range(2):
        for p in range(n_col):
            off = pl.multiple_of(place[p] * wa, wa)
            for i in range(ti):
                for k in range(nk):
                    at = (side * nk + k) * rank
                    row_full[i, at : at + rank, pl.ds(off, wa)] = rl[side][p][i, k]
        for p in range(n_row):
            off = pl.multiple_of(place[n_col + p] * wb, wb)
            for j in range(tj):
                for k in range(nk):
                    at = (side * nk + k) * rank
                    col_full[j, at : at + rank, pl.ds(off, wb)] = cl[side][p][j, k]
    for j in range(tj):
        csk[j] = dot1(sk[...], col_full[j], NT)
    for side in range(2):
        for k in range(nk):
            at = (side * nk + k) * rank
            for j in range(tj):
                m = dot6(
                    csk[j, :, at : at + rank], cpl[side][k, :, j * rank : (j + 1) * rank], NT
                )
                for i in range(ti):
                    mix[i, j * rank : (j + 1) * rank, at : at + rank] = m[
                        :, i * rank : (i + 1) * rank
                    ]
    for i in range(ti):
        update = dot3(mix[i], row_full[i])
        own = dot1(sk[...], tr[i].reshape(tj * rank, nb), NT)
        for j in range(tj):
            big[i * tj + j] = (
                dot3(own[:, j * rank : (j + 1) * rank], tl[i, j])
                - update[j * rank : (j + 1) * rank]
            )
    orthonormal_rows(big, work, ti * tj, rank)
    mine = pl.ds(pl.multiple_of(depth_at * half, half), half)
    for i in range(ti):
        parts = [big[i * tj + j, mine, :] for j in range(tj)]
        for j in range(tj):
            new_left[i, j] = parts[j] * math.sqrt(nb)
        basis_row = dot3(jnp.concatenate(parts, axis=0), row_full[i], NT)
        for side in range(2):
            for k in range(nk):
                at = (side * nk + k) * rank
                pr = dot6(
                    basis_row[:, at : at + rank], cpl[side][k, i * rank : (i + 1) * rank, :]
                )
                for j in range(tj):
                    proj[j, i * half : (i + 1) * half, at : at + rank] = pr[
                        j * half : (j + 1) * half, j * rank : (j + 1) * rank
                    ]
    for j in range(tj):
        update = dot3(proj[j], col_full[j])
        for i in range(ti):
            own = dot3(big[i * tj + j, mine, :], tl[i, j], NT)
            new_right[i, j] = (dot3(own, tr[i, j]) - update[i * half : (i + 1) * half]) * (
                1.0 / math.sqrt(nb)
            )


def swap(x, axis, mask):
    n = lax.axis_size(axis)
    return lax.ppermute(x, axis, [(i, i ^ mask) for i in range(n)])


def pieces_any(x, axis):
    n = lax.axis_size(axis)
    me = lax.axis_index(axis)
    if n & (n - 1) == 0:
        return [x] + [swap(x, axis, m) for m in range(1, n)], [me ^ m for m in range(n)]
    every = lax.all_gather(x, axis, axis=0)
    return [every[i] for i in range(n)], [jnp.int32(i) for i in range(n)]


def pieces_line4(x, axis):
    me = lax.axis_index(axis)
    ends = (me == 0) | (me == 3)
    near = lax.ppermute(x, axis, [(0, 1), (1, 0), (2, 3), (3, 2)])
    middle = lax.ppermute(x, axis, [(1, 2), (2, 1)])
    to_ends = lax.ppermute(middle, axis, [(1, 0), (2, 3)])
    far_middle = lax.ppermute(near, axis, [(1, 2), (2, 1)])
    far_ends = lax.ppermute(far_middle, axis, [(1, 0), (2, 3)])
    two = jnp.where(ends, to_ends, far_middle)
    three = jnp.where(ends, far_ends, middle)
    return [x, near, two, three], [me ^ m for m in range(4)]


def col_pieces(x):
    return (pieces_line4 if lax.axis_size("col") == 4 else pieces_any)(x, "col")


def vmem_call(kernel, outs, scratch, ins, n_smem):
    spec_s = pl.BlockSpec(memory_space=pltpu.MemorySpace.SMEM)
    spec_v = pl.BlockSpec(memory_space=pltpu.MemorySpace.VMEM)
    return pl.pallas_call(
        kernel,
        out_shape=outs,
        in_specs=[spec_s] * n_smem + [spec_v] * (len(ins) - n_smem),
        out_specs=jax.tree.map(lambda _: spec_v, outs),
        scratch_shapes=scratch,
        compiler_params=pltpu.CompilerParams(vmem_limit_bytes=56 << 20),
    )(*ins)


def on_device_pair(
    tile_left, tile_right, row_left, row_right, col_left, col_right, row_mask, col_mask, sketch
):
    ti, tj, rank, nb = tile_left.shape
    nk = row_left.shape[1]
    other = lambda x: swap(x, "depth", 1)
    rr, col_place = col_pieces(row_right)
    cr, row_place = pieces_any(col_right, "row")
    cl, _ = pieces_any(col_left, "row")
    rl, _ = col_pieces(row_left)
    n_col, n_row = len(rr), len(cr)
    place = jnp.stack([*col_place, *row_place, lax.axis_index("depth")]).astype(jnp.int32)
    coupling = vmem_call(
        functools.partial(coupling_kernel, n_col, n_row),
        jax.ShapeDtypeStruct((nk, ti * rank, tj * rank), F32),
        [pltpu.VMEM((nk, ti * rank, nb), BF16), pltpu.VMEM((nk, tj * rank, nb), BF16)],
        [place, row_mask, col_mask, *rr, *cr],
        3,
    )
    cl_other = [other(x) for x in cl]
    rl_other = [other(x) for x in rl]
    coupling_other = other(coupling)
    half = rank // 2
    out = jax.ShapeDtypeStruct((ti, tj, half, nb), F32)
    return vmem_call(
        functools.partial(tiles_kernel, n_col, n_row),
        (out, out),
        [
            pltpu.VMEM((ti, 2 * nk * rank, nb), BF16),
            pltpu.VMEM((tj, 2 * nk * rank, nb), BF16),
            pltpu.VMEM((tj, rank, 2 * nk * rank), F32),
            pltpu.VMEM((ti, tj * rank, 2 * nk * rank), F32),
            pltpu.VMEM((ti * tj, rank, nb), F32),
            pltpu.VMEM((ti * tj, rank, 2 * rank), F32),
            pltpu.VMEM((tj, ti * half, 2 * nk * rank), F32),
        ],
        [place, *rl, *rl_other, *cl, *cl_other, coupling, coupling_other, tile_left, tile_right, sketch],
        1,
    )


def orthonormalize(sketched):
    for repeat in range(2):
        gram_mat = jnp.einsum("ijtn,ijsn->ijts", sketched, sketched, precision=exact_mode)
        factor = jnp.linalg.cholesky(gram_mat)
        sketched = jax.scipy.linalg.solve_triangular(factor, sketched, lower=True)
    return sketched


def on_device_any(
    tile_left, tile_right, row_left, row_right, col_left, col_right, row_mask, col_mask, sketch
):
    rank, nb = sketch.shape
    exact = functools.partial(jnp.einsum, precision=exact_mode, preferred_element_type=F32)
    row_full_left, row_full_right = (
        lax.all_gather(row_left, "col", axis=3, tiled=True),
        lax.all_gather(row_right, "col", axis=3, tiled=True),
    )
    col_full_left, col_full_right = (
        lax.all_gather(col_left, "row", axis=3, tiled=True),
        lax.all_gather(col_right, "row", axis=3, tiled=True),
    )
    weight_table = row_mask.astype(F32)[:, None, :] * col_mask.astype(F32)[None, :, :]
    coupling = jnp.einsum(
        "ikrn,jksn->ijkrs", row_full_right, col_full_right, preferred_element_type=F32
    )
    coupling = coupling * weight_table[:, :, :, None, None]
    col_sketch = jnp.einsum("jksn,tn->jkst", col_full_left, sketch, preferred_element_type=F32)
    mixing = exact("ijkrs,jkst->ijkrt", coupling, col_sketch)
    partial_sketch = -exact("ijkrt,ikrn->ijtn", mixing, row_full_left)
    sketch_right = jnp.einsum("ijrn,tn->ijrt", tile_right, sketch, preferred_element_type=F32)
    summed = lax.psum(partial_sketch, "depth")
    sketched = summed + exact("ijrt,ijrn->ijtn", sketch_right, tile_left)
    basis = orthonormalize(sketched)
    rank_rows = rank // lax.axis_size("depth")
    rank_offset = lax.axis_index("depth") * rank_rows
    basis_mine = lax.dynamic_slice_in_dim(basis, rank_offset, rank_rows, 2)
    basis_row = exact("ijtn,ikrn->ijktr", basis, row_full_left)
    projected = exact("ijktr,ijkrs->ijkts", basis_row, coupling)
    right_part = -exact("ijkts,jksn->ijtn", projected, col_full_left)
    right_share = lax.psum_scatter(right_part, "depth", scatter_dimension=2, tiled=True)
    own_part = exact("ijtn,ijrn->ijtr", basis_mine, tile_left)
    right_share = right_share + exact("ijtr,ijrn->ijtn", own_part, tile_right)
    return (basis_mine * math.sqrt(nb), right_share / math.sqrt(nb))


def solution(mesh):
    in_specs = (
        P("row", "col", None, None),
        P("row", "col", None, None),
        P("row", "depth", None, "col"),
        P("row", "depth", None, "col"),
        P("col", "depth", None, "row"),
        P("col", "depth", None, "row"),
        P("row", "depth"),
        P("col", "depth"),
        P(),
    )
    out_specs = (P("row", "col", "depth", None), P("row", "col", "depth", None))
    body = on_device_pair if mesh.shape["depth"] == 2 else on_device_any
    return jax.shard_map(body, mesh=mesh, in_specs=in_specs, out_specs=out_specs, check_vma=False)
```
